32 devices in a mesh: pix: 8 (over y, x, core), chan: 4 (over z).
Axes of the slice: x: 2, y: 2, z: 4, core: 2. Of those that a mesh axis runs over, the one named last changes fastest.
Arguments:
- sky_map: bfloat16 [2048, 4096], P('pix', 'chan'), may hold values from -6 to 6
- channel_flags: int32 [4096], P('chan'), may hold values 0 or 1
- ripple_modes: int32 [4096], replicated, may hold values 0 or 1
- galaxy_block: int32 [128], P('pix'), may hold values from 0 to 127
- galaxy_offset: int32 [128], P('pix'), may hold values from 0 to 3968
- galaxy_weight: bfloat16 [128, 16, 128], P('pix'), may hold values from 0.099609375 to 10
Outputs:
- filtered: bfloat16 [2048, 4096], P(('pix', 'chan'))
- stack: float32 [16, 128], replicated
The draws below stay inside these ranges and needn't reach their ends.
All inputs are finite; a program needn't handle non-finite values. No bound on the sum of `channel_flags` on one device may be relied on, other than what follows from the above.
Results may differ from the reference program's by a relative error of at most 0.0051.
Values may be sent and summed in bfloat16 or wider, within the bound.
A program may use at most 128 MiB of HBM per device.

```python
import math
import jax
import jax.numpy as jnp
import numpy as np
from jax import lax

NCH = 4096
PB = 16
W = 128
PIXELS = 2048
BLOCKS = 128
NGAL = 128


def plant(result, own_key, least, top_value):
    dims = result.shape
    spot = [jax.random.randint(jax.random.fold_in(own_key, axis), (), 0, dims[axis]) for axis in range(len(dims))]
    result = result.at[tuple(spot)].set(least)
    longest = dims.index(max(dims))
    spot[longest] = (spot[longest] + 1) % dims[longest]
    return result.at[tuple(spot)].set(top_value)


def block_scale(own_key, dims, shards, low, high):
    gain, own = 1.0, jax.random.fold_in(own_key, 6)
    for position, blocks in shards:
        steps = jnp.exp(jax.random.uniform(jax.random.fold_in(own, position), (blocks,), jnp.float32, low / len(shards), high / len(shards)))
        gain = gain * jnp.repeat(steps, dims[position] // blocks).reshape([-1 if axis == position else 1 for axis in range(len(dims))])
    return gain


def rank_table(number_of, slope):
    weights = [(1 << 20) // math.isqrt(rank ** slope) + 1 for rank in range(1, number_of + 1)]
    deviation = 1 + sum(weights) // (1 << 30)
    return np.cumsum(np.array([max(1, weight // deviation) for weight in weights]))


def ranked(stream_key, shape, number_of, lean):
    listing = rank_table(number_of, lean)
    ticket = jax.random.randint(jax.random.fold_in(stream_key, 1), shape, 0, int(listing[number_of - 1]))
    standing = jnp.searchsorted(jnp.asarray(listing, jnp.int32), ticket, side="right")
    return jax.random.permutation(jax.random.fold_in(stream_key, 2), number_of)[standing].astype(jnp.int32)


def scatter_about(stream_key, shape, deviation, reach, cuts=(), kind=jnp.bfloat16):
    values = deviation * jax.random.normal(stream_key, shape, jnp.float32)
    if cuts:
        values = values * block_scale(stream_key, shape, cuts, -0.22, 0.18)
    return jnp.clip(values, -reach, reach).astype(kind)


def setup_inputs(seed: int = 0) -> dict:
    seeds = jax.random.split(jax.random.key(seed), 7)
    sky_map = scatter_about(seeds[0], (PIXELS, NCH), 1.0, 6.0, ((0, 8), (1, 4)))
    channel_flags = plant((jax.random.randint(seeds[1], (NCH,), 0, 8) < 7).astype(jnp.int32), jax.random.fold_in(seeds[1], 1), 0, 1)
    ripple_modes = plant((jax.random.randint(seeds[2], (NCH,), 0, 4) < 1).astype(jnp.int32), jax.random.fold_in(seeds[2], 1), 0, 1)
    galaxy_block = plant(ranked(seeds[3], (NGAL,), BLOCKS, 2), jax.random.fold_in(seeds[3], 3), 0, BLOCKS - 1).astype(jnp.int32)
    galaxy_offset = plant(jax.random.randint(seeds[4], (NGAL,), 0, NCH - W + 1), jax.random.fold_in(seeds[4], 1), 0, NCH - W).astype(jnp.int32)
    galaxy_weight = jnp.clip(jnp.exp(math.log(10.0) - 4.609084 * jax.random.uniform(seeds[5], (NGAL, PB, W), jnp.float32) ** block_scale(seeds[5], (NGAL, PB, W), ((0, 8),), -0.2, 0.2)), 0.099609375, 10.0).astype(jnp.bfloat16)
    return {"sky_map": sky_map, "channel_flags": channel_flags, "ripple_modes": ripple_modes, "galaxy_block": galaxy_block, "galaxy_offset": galaxy_offset, "galaxy_weight": galaxy_weight}


def basis_columns(total, start, count):
    rows = jnp.arange(total, dtype=jnp.int32)[:, None]
    cols = start + jnp.arange(count, dtype=jnp.int32)[None, :]
    half = total // 2
    is_cos = cols <= half
    mode = jnp.where(is_cos, cols, cols - half)
    phase = rows * mode % total
    angle = phase.astype(jnp.float32) * (2.0 * 3.141592653589793 / total)
    edge = jnp.logical_or(cols == 0, cols == half)
    factor = jnp.where(edge, (1.0 / total) ** 0.5, (2.0 / total) ** 0.5).astype(jnp.float32)
    value = jnp.where(is_cos, jnp.cos(angle), jnp.sin(angle)) * factor
    return value.astype(jnp.bfloat16)

def reference(sky_map, channel_flags, ripple_modes, galaxy_block, galaxy_offset, galaxy_weight):
    flagged = sky_map * channel_flags.astype(jnp.bfloat16)[None, :]
    basis = basis_columns(NCH, 0, NCH)
    coeffs = jnp.dot(flagged, basis, preferred_element_type=jnp.float32)
    kept = (coeffs * ripple_modes.astype(jnp.float32)[None, :]).astype(jnp.bfloat16)
    ripple = lax.dot_general(kept, basis, (((1,), (1,)), ((), ())), preferred_element_type=jnp.float32)
    filtered = (flagged.astype(jnp.float32) - ripple).astype(jnp.bfloat16)
    cube = filtered.reshape(BLOCKS, PB, NCH)

    def take(block, offset):
        zero = jnp.zeros((), jnp.int32)
        return lax.dynamic_slice(cube, (block.astype(jnp.int32), zero, offset.astype(jnp.int32)), (1, PB, W))[0]
    panels = jax.vmap(take)(galaxy_block, galaxy_offset).astype(jnp.float32)
    weights = galaxy_weight.astype(jnp.float32)
    numerator = lax.optimization_barrier(jnp.sum(weights * panels, axis=0))
    power = lax.optimization_barrier(jnp.sum(weights * weights, axis=0))
    return (filtered, numerator / jnp.sqrt(power))
```

```python
import functools
import math

import jax
import jax.numpy as jnp
import numpy as np
from jax import lax
from jax.experimental import pallas as pl
from jax.experimental.pallas import tpu as pltpu
from jax.sharding import PartitionSpec as P

MESH = pl.DeviceIdType.MESH
LANES = 128
SLABS = 32
TOTAL = LANES * SLABS
HALF = SLABS // 2
CHUNK = 16


def mode_table():
    col = np.arange(LANES)
    quarter, row = col // 32, col % 32
    is_sin, k2 = row // 16, 4 * (row % 16) + quarter
    lane = np.arange(LANES)[:, None]

    def half_block(k1):
        k = 32 * k2 + k1
        scale = np.full(LANES, math.sqrt(2.0 / TOTAL))
        phase = 2.0 * np.pi * ((lane * k[None, :]) % TOTAL) / TOTAL
        cos, sin = np.cos(phase), np.sin(phase)
        if k1 == 0:
            scale[k == 0] = math.sqrt(1.0 / TOTAL)
            edge = (is_sin == 1) & (k == 0)
            sin[:, edge] = np.where(lane % 2 == 0, 1.0, -1.0)
        return cos * scale, sin * scale

    def pick(a, b):
        return np.where(is_sin[None, :] == 1, b, a)

    blocks = np.zeros((HALF, 2 * LANES, 2 * LANES))
    for at, k1 in ((0, 0), (1, HALF)):
        cos, sin = half_block(k1)
        rows = slice(at * LANES, (at + 1) * LANES)
        blocks[0, rows, rows] = pick(cos, sin)
    for k1 in range(1, HALF):
        cos, sin = half_block(k1)
        blocks[k1, :LANES, :LANES] = pick(cos, sin)
        blocks[k1, LANES:, :LANES] = pick(sin, -cos)
        cos, sin = half_block(SLABS - k1)
        blocks[k1, :LANES, LANES:] = pick(cos, sin)
        blocks[k1, LANES:, LANES:] = pick(-sin, cos)
    return blocks.astype(jnp.bfloat16)


def times(value, c, s):
    re, im = value
    eps = 1e-12
    if abs(s) < eps and abs(c - 1) < eps:
        return value
    if abs(c) < eps and abs(s - 1) < eps:
        return (-im, re)
    if abs(c) < eps and abs(s + 1) < eps:
        return (im, -re)
    if abs(abs(c) - abs(s)) < eps:
        a = abs(c)
        sc, ss = math.copysign(1, c), math.copysign(1, s)
        t = re * (a * sc)
        u = im * (a * sc)
        return (t - u, u + t) if sc == ss else (t + u, u - t)
    return (re * c - im * s, re * s + im * c)


def real_forward(x):
    n = len(x)
    if n == 2:
        return [(x[0] + x[1], None), (x[0] - x[1], None)]
    even, odd = real_forward(x[0::2]), real_forward(x[1::2])
    half = n // 2
    out = [None] * (half + 1)
    for k in range(half // 2 + 1):
        e, o = even[k], odd[k]
        if k == 0:
            out[0] = (e[0] + o[0], None)
            out[half] = (e[0] - o[0], None)
        elif 2 * k == half:
            out[k] = (e[0], -o[0])
        else:
            angle = -2.0 * math.pi * k / n
            tr, ti = times(o, math.cos(angle), math.sin(angle))
            out[k] = (e[0] + tr, e[1] + ti)
            out[half - k] = (e[0] - tr, ti - e[1])
    return out


def real_inverse(z):
    half = len(z) - 1
    n = 2 * half
    if n == 2:
        return [z[0][0] + z[1][0], z[0][0] - z[1][0]]
    even, odd = [None] * (half // 2 + 1), [None] * (half // 2 + 1)
    for k in range(half // 2 + 1):
        a, b = z[k], z[half - k]
        if k == 0:
            even[0] = (a[0] + b[0], None)
            odd[0] = (a[0] - b[0], None)
        elif 2 * k == half:
            even[k] = (a[0] + a[0], None)
            odd[k] = (-(a[1] + a[1]), None)
        else:
            angle = 2.0 * math.pi * k / n
            even[k] = (a[0] + b[0], a[1] - b[1])
            odd[k] = times((a[0] - b[0], a[1] + b[1]), math.cos(angle), math.sin(angle))
    out = [None] * n
    out[0::2] = real_inverse(even)
    out[1::2] = real_inverse(odd)
    return out


def kernel(
    pix, chan, sky_ref, flags_ref, modes_ref, block_ref, offset_ref, weight_ref, table_ref,
    out_ref, stack_ref,
    lines, flags, weights, meta, meta_own, meta_smem, table, spec, back, cube, staged, part, sums, part2, sums2,
    flag_f, local_sem, line_send, line_recv, flag_send, flag_recv, w_send, w_recv, m_send, m_recv, s_send, s_recv,
    t_send, t_recv,
):
    me_p, me_c = lax.axis_index("pix"), lax.axis_index("chan")
    rows = lines.shape[1]
    per = SLABS // chan
    count = weights.shape[1]
    patch = weights.shape[2]

    own = [
        pltpu.make_async_copy(table_ref, table, local_sem.at[0]),
        pltpu.make_async_copy(sky_ref.at[pl.ds(pl.multiple_of(me_c * rows, rows), rows)], lines.at[me_c], local_sem.at[1]),
        pltpu.make_async_copy(flags_ref, flags.at[me_c], local_sem.at[2]),
        pltpu.make_async_copy(weight_ref, weights.at[me_p], local_sem.at[3]),
    ]
    for copy in own:
        copy.start()
    meta_own[0:1, 0:count] = block_ref[...]
    meta_own[1:2, 0:count] = offset_ref[...]

    barrier = pltpu.get_barrier_semaphore()
    chan_peers = [lax.rem(me_c + d, chan) for d in range(1, chan)]
    pix_peers = [lax.rem(me_p + d, pix) for d in range(1, pix)]
    for c in chan_peers:
        pl.semaphore_signal(barrier, inc=1, device_id=(me_p, c), device_id_type=MESH)
    for p in pix_peers:
        pl.semaphore_signal(barrier, inc=1, device_id=(p, me_c), device_id_type=MESH)
    pl.semaphore_wait(barrier, chan + pix - 2)

    def remote(src, dst, send, recv, device):
        return pltpu.make_async_remote_copy(
            src_ref=src, dst_ref=dst, send_sem=send, recv_sem=recv, device_id=device, device_id_type=MESH
        )

    line_copies, flag_copies, w_copies, m_copies = [], [], [], []
    for i, c in enumerate(chan_peers):
        line_copies.append(
            remote(
                sky_ref.at[pl.ds(pl.multiple_of(c * rows, rows), rows)], lines.at[me_c],
                line_send.at[i], line_recv.at[i], (me_p, c),
            )
        )
        line_copies[-1].start()
    for i, p in enumerate(pix_peers):
        m_copies.append(remote(meta_own, meta.at[me_p], m_send.at[i], m_recv.at[i], (p, me_c)))
        m_copies[-1].start()
        w_copies.append(remote(weight_ref, weights.at[me_p], w_send.at[i], w_recv.at[i], (p, me_c)))
        w_copies[-1].start()
    for i, c in enumerate(chan_peers):
        flag_copies.append(remote(flags_ref, flags.at[me_c], flag_send.at[i], flag_recv.at[i], (me_p, c)))
        flag_copies[-1].start()

    modes = modes_ref[...].astype(jnp.float32)
    eye = (
        lax.broadcasted_iota(jnp.int32, (LANES, LANES), 0) == lax.broadcasted_iota(jnp.int32, (LANES, LANES), 1)
    ).astype(jnp.float32)
    turned = lax.dot_general(eye, modes, (((1,), (1,)), ((), ())), preferred_element_type=jnp.float32)
    mask = jnp.zeros((32, LANES), jnp.float32)
    for q in range(4):
        place = (
            lax.broadcasted_iota(jnp.int32, (32, LANES), 1) == lax.broadcasted_iota(jnp.int32, (32, LANES), 0) + 32 * q
        ).astype(jnp.float32)
        mask = mask + jnp.dot(turned[32 * q : 32 * q + 32], place, preferred_element_type=jnp.float32)

    meta[me_p] = meta_own[...]
    for copy in m_copies:
        copy.wait()
    to_smem = pltpu.make_async_copy(meta, meta_smem, local_sem.at[4])
    to_smem.start()
    for copy in own:
        copy.wait()
    for copy in w_copies:
        copy.wait()
    to_smem.wait()

    def add_power(i, acc):
        w = weights[i].astype(jnp.float32)
        return acc + jnp.sum(w * w, axis=0)

    power = lax.fori_loop(0, pix, add_power, jnp.zeros((patch, LANES), jnp.float32))

    for copy in flag_copies:
        copy.wait()
    for c in range(chan):
        flag_f[c * per : (c + 1) * per, :] = flags[c].astype(jnp.float32)
    for copy in line_copies:
        copy.wait()

    def slab(n1, at):
        c, s = n1 // per, n1 % per
        value = lines[c, pl.ds(at, CHUNK), s * LANES : (s + 1) * LANES].astype(jnp.float32)
        return value * flag_f[n1 : n1 + 1, :]

    def forward(i, carry):
        at = pl.multiple_of(i * CHUNK, CHUNK)
        y = real_forward([slab(n1, at) for n1 in range(SLABS)])
        spec[0, pl.ds(at, CHUNK), :LANES] = y[0][0].astype(jnp.bfloat16)
        spec[0, pl.ds(at, CHUNK), LANES:] = y[HALF][0].astype(jnp.bfloat16)
        for k in range(1, HALF):
            spec[k, pl.ds(at, CHUNK), :LANES] = y[k][0].astype(jnp.bfloat16)
            spec[k, pl.ds(at, CHUNK), LANES:] = y[k][1].astype(jnp.bfloat16)
        return carry

    lax.fori_loop(0, rows // CHUNK, forward, 0)

    for k in range(HALF):
        other = HALF if k == 0 else SLABS - k
        gain = 1.0 if k == 0 else 0.5
        chosen = jnp.concatenate([mask[k : k + 1], mask[other : other + 1]], axis=1) * gain
        coeffs = jnp.dot(spec[k], table[k], preferred_element_type=jnp.float32)
        kept = (coeffs * chosen).astype(jnp.bfloat16)
        back[k] = lax.dot_general(kept, table[k], (((1,), (1,)), ((), ())), preferred_element_type=jnp.float32)

    def inverse(i, carry):
        at = pl.multiple_of(i * CHUNK, CHUNK)
        here = pl.ds(at, CHUNK)
        z = [(back[0, here, :LANES], None)]
        z += [(back[k, here, :LANES], back[k, here, LANES:]) for k in range(1, HALF)]
        z += [(back[0, here, LANES:], None)]
        ripple = real_inverse(z)
        for n1 in range(SLABS):
            value = (slab(n1, at) - ripple[n1]).astype(jnp.bfloat16)
            staged[here, n1 * LANES : (n1 + 1) * LANES] = value
            cube[i * SLABS + n1] = value.astype(jnp.float32)
        return carry

    lax.fori_loop(0, rows // CHUNK, inverse, 0)
    result = pltpu.make_async_copy(staged, out_ref, local_sem.at[5])
    result.start()

    here_blocks = rows // patch
    first = (me_p * chan + me_c) * here_blocks
    lane = lax.broadcasted_iota(jnp.int32, (patch, LANES), 1)

    def add_panels(p, acc):
        for g in range(count):
            local = meta_smem[p, 0, g] - first
            offset = meta_smem[p, 1, g]
            safe = jnp.clip(local, 0, here_blocks - 1)
            owned = local == safe
            base = offset // LANES
            shift = offset - base * LANES
            low = cube[safe * SLABS + base]
            high = cube[safe * SLABS + jnp.minimum(base + 1, SLABS - 1)]
            joined = jnp.where(lane >= shift, low, high)
            panel = pltpu.roll(joined, lax.rem(LANES - shift, LANES), 1)
            w = weights[p, g].astype(jnp.float32)
            acc = acc + jnp.where(owned, w * panel, 0.0)
        return acc

    total = lax.fori_loop(0, pix, add_panels, jnp.zeros((patch, LANES), jnp.float32))

    part[...] = total
    sends = [
        remote(part, sums.at[me_p], s_send.at[i], s_recv.at[i], (p, me_c)) for i, p in enumerate(pix_peers)
    ]
    for copy in sends:
        copy.start()
    sums[me_p] = total
    for copy in sends:
        copy.wait()
    total = jnp.sum(sums[...], axis=0)
    part2[...] = total
    sends = [
        remote(part2, sums2.at[me_c], t_send.at[i], t_recv.at[i], (me_p, c)) for i, c in enumerate(chan_peers)
    ]
    for copy in sends:
        copy.start()
    sums2[me_c] = total
    for copy in sends:
        copy.wait()
    stack_ref[...] = jnp.sum(sums2[...], axis=0) / jnp.sqrt(power)
    result.wait()


def solution(mesh):
    pix, chan = mesh.shape["pix"], mesh.shape["chan"]

    def body(sky_map, channel_flags, ripple_modes, galaxy_block, galaxy_offset, galaxy_weight):
        rows = sky_map.shape[0] // chan
        width = sky_map.shape[1]
        count, patch, _ = galaxy_weight.shape
        per = width // LANES
        any_spec = pl.BlockSpec(memory_space=pl.ANY)
        vmem_spec = pl.BlockSpec(memory_space=pltpu.VMEM)
        dma = pltpu.SemaphoreType.DMA
        table = jnp.asarray(mode_table())
        return pl.pallas_call(
            functools.partial(kernel, pix, chan),
            out_shape=(
                jax.ShapeDtypeStruct((rows, TOTAL), jnp.bfloat16),
                jax.ShapeDtypeStruct((patch, LANES), jnp.float32),
            ),
            in_specs=[any_spec, any_spec, vmem_spec, vmem_spec, vmem_spec, any_spec, any_spec],
            out_specs=(any_spec, vmem_spec),
            scratch_shapes=[
                pltpu.VMEM((chan, rows, width), jnp.bfloat16),
                pltpu.VMEM((chan, per, LANES), jnp.int32),
                pltpu.VMEM((pix, count, patch, LANES), jnp.bfloat16),
                pltpu.VMEM((pix, 8, LANES), jnp.int32),
                pltpu.VMEM((8, LANES), jnp.int32),
                pltpu.SMEM((pix, 8, LANES), jnp.int32),
                pltpu.VMEM((HALF, 2 * LANES, 2 * LANES), jnp.bfloat16),
                pltpu.VMEM((HALF, rows, 2 * LANES), jnp.bfloat16),
                pltpu.VMEM((HALF, rows, 2 * LANES), jnp.float32),
                pltpu.VMEM((rows // patch * SLABS, patch, LANES), jnp.float32),
                pltpu.VMEM((rows, TOTAL), jnp.bfloat16),
                pltpu.VMEM((patch, LANES), jnp.float32),
                pltpu.VMEM((pix, patch, LANES), jnp.float32),
                pltpu.VMEM((patch, LANES), jnp.float32),
                pltpu.VMEM((chan, patch, LANES), jnp.float32),
                pltpu.VMEM((SLABS, LANES), jnp.float32),
                dma((6,)),
                dma((chan - 1,)), dma((chan - 1,)), dma((chan - 1,)), dma((chan - 1,)),
                dma((pix - 1,)), dma((pix - 1,)), dma((pix - 1,)), dma((pix - 1,)),
                dma((pix - 1,)), dma((pix - 1,)),
                dma((chan - 1,)), dma((chan - 1,)),
            ],
            compiler_params=pltpu.CompilerParams(collective_id=0, has_side_effects=True),
        )(
            sky_map, channel_flags.reshape(per, LANES), ripple_modes.reshape(32, LANES),
            galaxy_block.reshape(1, count), galaxy_offset.reshape(1, count), galaxy_weight, table,
        )

    in_specs = (P("pix", "chan"), P("chan"), P(), P("pix"), P("pix"), P("pix", None, None))
    out_specs = (P(("pix", "chan"), None), P())
    return jax.shard_map(body, mesh=mesh, in_specs=in_specs, out_specs=out_specs, check_vma=False)
```

```python
import functools
import math

import jax
import jax.numpy as jnp
import numpy as np
from jax import lax
from jax.experimental import pallas as pl
from jax.experimental.pallas import tpu as pltpu
from jax.sharding import PartitionSpec as P

MESH = pl.DeviceIdType.MESH
LANES = 128
SLABS = 32
TOTAL = LANES * SLABS
HALF = SLABS // 2
CHUNK = 16
STEP = 16


def mode_table():
    col = np.arange(LANES)
    quarter, row = col // 32, col % 32
    is_sin, k2 = row // 16, 4 * (row % 16) + quarter
    lane = np.arange(LANES)[:, None]

    def half_block(k1):
        k = 32 * k2 + k1
        scale = np.full(LANES, math.sqrt(2.0 / TOTAL))
        phase = 2.0 * np.pi * ((lane * k[None, :]) % TOTAL) / TOTAL
        cos, sin = np.cos(phase), np.sin(phase)
        if k1 == 0:
            scale[k == 0] = math.sqrt(1.0 / TOTAL)
            edge = (is_sin == 1) & (k == 0)
            sin[:, edge] = np.where(lane % 2 == 0, 1.0, -1.0)
        return cos * scale, sin * scale

    def pick(a, b):
        return np.where(is_sin[None, :] == 1, b, a)

    blocks = np.zeros((HALF, 2 * LANES, 2 * LANES))
    for at, k1 in ((0, 0), (1, HALF)):
        cos, sin = half_block(k1)
        rows = slice(at * LANES, (at + 1) * LANES)
        blocks[0, rows, rows] = pick(cos, sin)
    for k1 in range(1, HALF):
        cos, sin = half_block(k1)
        blocks[k1, :LANES, :LANES] = pick(cos, sin)
        blocks[k1, LANES:, :LANES] = pick(sin, -cos)
        cos, sin = half_block(SLABS - k1)
        blocks[k1, :LANES, LANES:] = pick(cos, sin)
        blocks[k1, LANES:, LANES:] = pick(-sin, cos)
    return blocks.astype(jnp.bfloat16)


def times(value, c, s):
    re, im = value
    eps = 1e-12
    if abs(s) < eps and abs(c - 1) < eps:
        return value
    if abs(c) < eps and abs(s - 1) < eps:
        return (-im, re)
    if abs(c) < eps and abs(s + 1) < eps:
        return (im, -re)
    if abs(abs(c) - abs(s)) < eps:
        a = abs(c)
        sc, ss = math.copysign(1, c), math.copysign(1, s)
        t = re * (a * sc)
        u = im * (a * sc)
        return (t - u, u + t) if sc == ss else (t + u, u - t)
    return (re * c - im * s, re * s + im * c)


def real_forward(x):
    n = len(x)
    if n == 2:
        return [(x[0] + x[1], None), (x[0] - x[1], None)]
    even, odd = real_forward(x[0::2]), real_forward(x[1::2])
    half = n // 2
    out = [None] * (half + 1)
    for k in range(half // 2 + 1):
        e, o = even[k], odd[k]
        if k == 0:
            out[0] = (e[0] + o[0], None)
            out[half] = (e[0] - o[0], None)
        elif 2 * k == half:
            out[k] = (e[0], -o[0])
        else:
            angle = -2.0 * math.pi * k / n
            tr, ti = times(o, math.cos(angle), math.sin(angle))
            out[k] = (e[0] + tr, e[1] + ti)
            out[half - k] = (e[0] - tr, ti - e[1])
    return out


def real_inverse(z):
    half = len(z) - 1
    n = 2 * half
    if n == 2:
        return [z[0][0] + z[1][0], z[0][0] - z[1][0]]
    even, odd = [None] * (half // 2 + 1), [None] * (half // 2 + 1)
    for k in range(half // 2 + 1):
        a, b = z[k], z[half - k]
        if k == 0:
            even[0] = (a[0] + b[0], None)
            odd[0] = (a[0] - b[0], None)
        elif 2 * k == half:
            even[k] = (a[0] + a[0], None)
            odd[k] = (-(a[1] + a[1]), None)
        else:
            angle = 2.0 * math.pi * k / n
            even[k] = (a[0] + b[0], a[1] - b[1])
            odd[k] = times((a[0] - b[0], a[1] + b[1]), math.cos(angle), math.sin(angle))
    out = [None] * n
    out[0::2] = real_inverse(even)
    out[1::2] = real_inverse(odd)
    return out


def kernel(
    pix, chan, sky_ref, flags_ref, modes_ref, block_ref, offset_ref, weight_ref, table_ref,
    out_ref, stack_ref,
    lines, flags, modes_v, block_v, offset_v, weights, chosen_w, meta, meta_own, meta_smem, table, spec, back, cube, staged,
    part, sums, part2, sums2, flag_f, mask_ref, local_sem, out_sem, line_send, line_recv, flag_send, flag_recv,
    w_send, w_recv, m_send, m_recv, s_send, s_recv, t_send, t_recv,
):
    me_p, me_c = lax.axis_index("pix"), lax.axis_index("chan")
    rows = lines.shape[1]
    per = SLABS // chan
    count = weights.shape[1]
    patch = weights.shape[2]
    steps = rows // STEP

    barrier = pltpu.get_barrier_semaphore()
    chan_peers = [lax.rem(me_c + d, chan) for d in range(1, chan)]
    pix_peers = [lax.rem(me_p + d, pix) for d in range(1, pix)]
    for c in chan_peers:
        pl.semaphore_signal(barrier, inc=1, device_id=(me_p, c), device_id_type=MESH)
    for p in pix_peers:
        pl.semaphore_signal(barrier, inc=1, device_id=(p, me_c), device_id_type=MESH)

    own = [
        pltpu.make_async_copy(table_ref, table, local_sem.at[0]),
        pltpu.make_async_copy(sky_ref.at[pl.ds(pl.multiple_of(me_c * rows, rows), rows)], lines.at[me_c], local_sem.at[1]),
        pltpu.make_async_copy(flags_ref, flags.at[me_c], local_sem.at[2]),
        pltpu.make_async_copy(weight_ref, weights.at[me_p], local_sem.at[3]),
        pltpu.make_async_copy(modes_ref, modes_v, local_sem.at[5]),
    ]
    places = [
        pltpu.make_async_copy(block_ref, block_v, local_sem.at[6]),
        pltpu.make_async_copy(offset_ref, offset_v, local_sem.at[7]),
    ]
    for copy in places + own:
        copy.start()
    for copy in places:
        copy.wait()
    meta_own[0:1, 0:count] = block_v[...]
    meta_own[1:2, 0:count] = offset_v[...]
    pl.semaphore_wait(barrier, chan + pix - 2)

    def remote(src, dst, send, recv, device):
        return pltpu.make_async_remote_copy(
            src_ref=src, dst_ref=dst, send_sem=send, recv_sem=recv, device_id=device, device_id_type=MESH
        )

    def line_copy(i, c, step):
        there = pl.ds(pl.multiple_of(c * rows + step * STEP, STEP), STEP)
        here = pl.ds(pl.multiple_of(step * STEP, STEP), STEP)
        return remote(
            sky_ref.at[there], lines.at[me_c, here], line_send.at[step, i], line_recv.at[step, i], (me_p, c)
        )

    flag_copies, w_copies, m_copies = [], [], []
    for step in range(steps):
        for i, c in enumerate(chan_peers):
            if step == 0:
                flag_copies.append(remote(flags_ref, flags.at[me_c], flag_send.at[i], flag_recv.at[i], (me_p, c)))
                flag_copies[-1].start()
            line_copy(i, c, step).start()
    for i, p in enumerate(pix_peers):
        m_copies.append(remote(meta_own, meta.at[me_p], m_send.at[i], m_recv.at[i], (p, me_c)))
        m_copies[-1].start()
        w_copies.append(remote(weight_ref, weights.at[me_p], w_send.at[i], w_recv.at[i], (p, me_c)))
        w_copies[-1].start()

    for copy in own:
        copy.wait()
    modes = modes_v[...].astype(jnp.float32)
    eye = (
        lax.broadcasted_iota(jnp.int32, (LANES, LANES), 0) == lax.broadcasted_iota(jnp.int32, (LANES, LANES), 1)
    ).astype(jnp.float32)
    turned = lax.dot_general(eye, modes, (((1,), (1,)), ((), ())), preferred_element_type=jnp.float32)
    mask = jnp.zeros((32, LANES), jnp.float32)
    for q in range(4):
        place = (
            lax.broadcasted_iota(jnp.int32, (32, LANES), 1) == lax.broadcasted_iota(jnp.int32, (32, LANES), 0) + 32 * q
        ).astype(jnp.float32)
        mask = mask + jnp.dot(turned[32 * q : 32 * q + 32], place, preferred_element_type=jnp.float32)
    mask_ref[...] = mask

    for copy in flag_copies:
        copy.wait()
    for c in range(chan):
        flag_f[c * per : (c + 1) * per, :] = flags[c].astype(jnp.float32)

    meta[me_p] = meta_own[...]
    for copy in m_copies:
        copy.wait()
    to_smem = pltpu.make_async_copy(meta, meta_smem, local_sem.at[4])
    to_smem.start()
    for copy in w_copies:
        copy.wait()
    to_smem.wait()

    here_blocks = rows // patch
    first = (me_p * chan + me_c) * here_blocks

    def choose(p, acc):
        for g in range(count):
            local = meta_smem[p, 0, g] - first
            safe = jnp.clip(local, 0, here_blocks - 1)
            offset = meta_smem[p, 1, g]
            base = lax.div(offset, LANES)
            shift = offset - base * LANES
            meta_smem[p, 2, g] = safe * SLABS + base
            meta_smem[p, 3, g] = safe * SLABS + jnp.minimum(base + 1, SLABS - 1)
            meta_smem[p, 4, g] = shift
            w = weights[p, g].astype(jnp.float32)
            acc = acc + w * w
            chosen_w[p, g] = jnp.where(local == safe, w, 0.0)
        return acc

    power = lax.fori_loop(0, pix, choose, jnp.zeros((patch, LANES), jnp.float32))

    def slab(n1, at):
        c, s = n1 // per, n1 % per
        value = lines[c, pl.ds(at, CHUNK), s * LANES : (s + 1) * LANES].astype(jnp.float32)
        return value * flag_f[n1 : n1 + 1, :]

    def filter_rows(step, carry):
        for i, c in enumerate(chan_peers):
            line_copy(i, c, step).wait_recv()
        for j in range(STEP // CHUNK):
            at = pl.multiple_of(step * STEP + j * CHUNK, CHUNK)
            r = slice(j * CHUNK, (j + 1) * CHUNK)
            y = real_forward([slab(n1, at) for n1 in range(SLABS)])
            spec[0, r, :LANES] = y[0][0].astype(jnp.bfloat16)
            spec[0, r, LANES:] = y[HALF][0].astype(jnp.bfloat16)
            for k in range(1, HALF):
                spec[k, r, :LANES] = y[k][0].astype(jnp.bfloat16)
                spec[k, r, LANES:] = y[k][1].astype(jnp.bfloat16)
        for k in range(HALF):
            other = HALF if k == 0 else SLABS - k
            gain = 1.0 if k == 0 else 0.5
            chosen = jnp.concatenate([mask_ref[k : k + 1], mask_ref[other : other + 1]], axis=1) * gain
            coeffs = jnp.dot(spec[k], table[k], preferred_element_type=jnp.float32)
            kept = (coeffs * chosen).astype(jnp.bfloat16)
            back[k] = lax.dot_general(kept, table[k], (((1,), (1,)), ((), ())), preferred_element_type=jnp.float32)
        for j in range(STEP // CHUNK):
            at = pl.multiple_of(step * STEP + j * CHUNK, CHUNK)
            r = slice(j * CHUNK, (j + 1) * CHUNK)
            z = [(back[0, r, :LANES], None)]
            z += [(back[k, r, :LANES], back[k, r, LANES:]) for k in range(1, HALF)]
            z += [(back[0, r, LANES:], None)]
            ripple = real_inverse(z)
            for n1 in range(SLABS):
                value = (slab(n1, at) - ripple[n1]).astype(jnp.bfloat16)
                staged[pl.ds(at, CHUNK), n1 * LANES : (n1 + 1) * LANES] = value
                cube[(step * (STEP // CHUNK) + j) * SLABS + n1] = value.astype(jnp.float32)
        here = pl.ds(pl.multiple_of(step * STEP, STEP), STEP)
        pltpu.make_async_copy(staged.at[here], out_ref.at[here], out_sem.at[step]).start()
        return carry

    lax.fori_loop(0, steps, filter_rows, 0)

    lane = lax.broadcasted_iota(jnp.int32, (patch, LANES), 1)

    def add_panels(p, acc):
        for g in range(count):
            low = cube[meta_smem[p, 2, g]]
            high = cube[meta_smem[p, 3, g]]
            shift = meta_smem[p, 4, g]
            joined = jnp.where(lane >= shift, low, high)
            panel = pltpu.roll(joined, lax.rem(LANES - shift, LANES), 1)
            acc = acc + chosen_w[p, g] * panel
        return acc

    total = lax.fori_loop(0, pix, add_panels, jnp.zeros((patch, LANES), jnp.float32))

    part[...] = total
    sends = [
        remote(part, sums.at[me_p], s_send.at[i], s_recv.at[i], (p, me_c)) for i, p in enumerate(pix_peers)
    ]
    for copy in sends:
        copy.start()
    sums[me_p] = total
    for copy in sends:
        copy.wait()
    total = jnp.sum(sums[...], axis=0)
    part2[...] = total
    sends = [
        remote(part2, sums2.at[me_c], t_send.at[i], t_recv.at[i], (me_p, c)) for i, c in enumerate(chan_peers)
    ]
    for copy in sends:
        copy.start()
    sums2[me_c] = total
    for step in range(steps):
        for i, c in enumerate(chan_peers):
            line_copy(i, c, step).wait_send()
        here = pl.ds(step * STEP, STEP)
        pltpu.make_async_copy(staged.at[here], out_ref.at[here], out_sem.at[step]).wait()
    for copy in sends:
        copy.wait()
    stack_ref[...] = jnp.sum(sums2[...], axis=0) / jnp.sqrt(power)


def hand_over(filtered_ref, stack_ref, out_ref, stack_out, sem):
    copy = pltpu.make_async_copy(filtered_ref, out_ref, sem)
    copy.start()
    stack_out[...] = stack_ref[...]
    copy.wait()


def solution(mesh):
    pix, chan = mesh.shape["pix"], mesh.shape["chan"]

    def body(sky_map, channel_flags, ripple_modes, galaxy_block, galaxy_offset, galaxy_weight):
        rows = sky_map.shape[0] // chan
        width = sky_map.shape[1]
        count, patch, _ = galaxy_weight.shape
        per = width // LANES
        any_spec = pl.BlockSpec(memory_space=pl.ANY)
        vmem_spec = pl.BlockSpec(memory_space=pltpu.VMEM)
        dma = pltpu.SemaphoreType.DMA
        table = jnp.asarray(mode_table())
        shapes = (
            jax.ShapeDtypeStruct((rows, TOTAL), jnp.bfloat16),
            jax.ShapeDtypeStruct((patch, LANES), jnp.float32),
        )
        filtered, stack = pl.pallas_call(
            functools.partial(kernel, pix, chan),
            out_shape=shapes,
            in_specs=[pl.BlockSpec(memory_space=pltpu.HBM)] * 7,
            out_specs=(any_spec, vmem_spec),
            scratch_shapes=[
                pltpu.VMEM((chan, rows, width), jnp.bfloat16),
                pltpu.VMEM((chan, per, LANES), jnp.int32),
                pltpu.VMEM((32, LANES), jnp.int32),
                pltpu.VMEM((1, count), jnp.int32),
                pltpu.VMEM((1, count), jnp.int32),
                pltpu.VMEM((pix, count, patch, LANES), jnp.bfloat16),
                pltpu.VMEM((pix, count, patch, LANES), jnp.float32),
                pltpu.VMEM((pix, 8, LANES), jnp.int32),
                pltpu.VMEM((8, LANES), jnp.int32),
                pltpu.SMEM((pix, 8, LANES), jnp.int32),
                pltpu.VMEM((HALF, 2 * LANES, 2 * LANES), jnp.bfloat16),
                pltpu.VMEM((HALF, STEP, 2 * LANES), jnp.bfloat16),
                pltpu.VMEM((HALF, STEP, 2 * LANES), jnp.float32),
                pltpu.VMEM((rows // patch * SLABS, patch, LANES), jnp.float32),
                pltpu.VMEM((rows, TOTAL), jnp.bfloat16),
                pltpu.VMEM((patch, LANES), jnp.float32),
                pltpu.VMEM((pix, patch, LANES), jnp.float32),
                pltpu.VMEM((patch, LANES), jnp.float32),
                pltpu.VMEM((chan, patch, LANES), jnp.float32),
                pltpu.VMEM((SLABS, LANES), jnp.float32),
                pltpu.VMEM((SLABS, LANES), jnp.float32),
                dma((8,)), dma((rows // STEP,)),
                dma((rows // STEP, chan - 1)), dma((rows // STEP, chan - 1)), dma((chan - 1,)), dma((chan - 1,)),
                dma((pix - 1,)), dma((pix - 1,)), dma((pix - 1,)), dma((pix - 1,)),
                dma((pix - 1,)), dma((pix - 1,)),
                dma((chan - 1,)), dma((chan - 1,)),
            ],
            compiler_params=pltpu.CompilerParams(collective_id=0, has_side_effects=True, vmem_limit_bytes=32 << 20),
        )(
            *(pltpu.with_memory_space_constraint(v, pltpu.HBM) for v in (
            sky_map, channel_flags.reshape(per, LANES), ripple_modes.reshape(32, LANES),
            galaxy_block.reshape(1, count), galaxy_offset.reshape(1, count), galaxy_weight, table,
            ))
        )
        return pl.pallas_call(
            hand_over,
            out_shape=shapes,
            in_specs=[any_spec, vmem_spec],
            out_specs=(any_spec, vmem_spec),
            scratch_shapes=[dma(())],
            compiler_params=pltpu.CompilerParams(vmem_limit_bytes=2 << 20),
        )(filtered, stack)

    in_specs = (P("pix", "chan"), P("chan"), P(), P("pix"), P("pix"), P("pix", None, None))
    out_specs = (P(("pix", "chan"), None), P())
    return jax.shard_map(body, mesh=mesh, in_specs=in_specs, out_specs=out_specs, check_vma=False)
```

```python
import functools
import math

import jax
import jax.numpy as jnp
import numpy as np
from jax import lax
from jax.experimental import pallas as pl
from jax.experimental.pallas import tpu as pltpu
from jax.sharding import PartitionSpec as P

MESH = pl.DeviceIdType.MESH
LANES = 128
SLABS = 32
TOTAL = LANES * SLABS
HALF = SLABS // 2
CHUNK = 16
STEP = 16


def mode_tables():
    col = np.arange(LANES)
    quarter, row = col // 32, col % 32
    is_sin, k2 = (row // 16 == 1)[None, :], 4 * (row % 16) + quarter
    lane = np.arange(LANES)[:, None]

    def waves(k):
        phase = 2.0 * np.pi * ((lane * k[None, :]) % TOTAL) / TOTAL
        return np.cos(phase) * math.sqrt(2.0 / TOTAL), np.sin(phase) * math.sqrt(2.0 / TOTAL)

    tables = np.zeros((4, 2 * LANES, 2 * LANES))
    cos, sin = waves(32 * k2)
    cos[:, k2 == 0] *= math.sqrt(0.5)
    sin[:, k2 == 0] = np.where(lane % 2 == 0, 1.0, -1.0) * math.sqrt(1.0 / TOTAL)
    tables[0, :LANES, :LANES] = np.where(is_sin, sin, cos)
    cos, sin = waves(32 * k2 + 16)
    tables[0, LANES:, LANES:] = np.where(is_sin, sin, cos)
    cos, sin = waves(32 * k2)
    tables[1, :LANES, :LANES] = np.where(is_sin, sin, cos)
    tables[1, LANES:, :LANES] = np.where(is_sin, -cos, sin)
    cos, sin = waves(32 * (LANES - 1 - k2))
    tables[1, :LANES, LANES:] = np.where(is_sin, -sin, cos)
    tables[1, LANES:, LANES:] = np.where(is_sin, cos, sin)
    tables[2], tables[3] = tables[0].T, tables[1].T
    phase = 2.0 * np.pi * np.arange(HALF)[:, None] * np.arange(LANES)[None, :] / TOTAL
    return tables.astype(jnp.bfloat16), np.concatenate([np.cos(phase), np.sin(phase)]).astype(np.float32)


def times(value, c, s):
    re, im = value
    eps = 1e-12
    if abs(s) < eps and abs(c - 1) < eps:
        return value
    if abs(c) < eps and abs(s - 1) < eps:
        return (-im, re)
    if abs(c) < eps and abs(s + 1) < eps:
        return (im, -re)
    if abs(abs(c) - abs(s)) < eps:
        a = abs(c)
        sc, ss = math.copysign(1, c), math.copysign(1, s)
        t = re * (a * sc)
        u = im * (a * sc)
        return (t - u, u + t) if sc == ss else (t + u, u - t)
    return (re * c - im * s, re * s + im * c)


def real_forward(x):
    n = len(x)
    if n == 2:
        return [(x[0] + x[1], None), (x[0] - x[1], None)]
    even, odd = real_forward(x[0::2]), real_forward(x[1::2])
    half = n // 2
    out = [None] * (half + 1)
    for k in range(half // 2 + 1):
        e, o = even[k], odd[k]
        if k == 0:
            out[0] = (e[0] + o[0], None)
            out[half] = (e[0] - o[0], None)
        elif 2 * k == half:
            out[k] = (e[0], -o[0])
        else:
            angle = -2.0 * math.pi * k / n
            tr, ti = times(o, math.cos(angle), math.sin(angle))
            out[k] = (e[0] + tr, e[1] + ti)
            out[half - k] = (e[0] - tr, ti - e[1])
    return out


def real_inverse(z):
    half = len(z) - 1
    n = 2 * half
    if n == 2:
        return [z[0][0] + z[1][0], z[0][0] - z[1][0]]
    even, odd = [None] * (half // 2 + 1), [None] * (half // 2 + 1)
    for k in range(half // 2 + 1):
        a, b = z[k], z[half - k]
        if k == 0:
            even[0] = (a[0] + b[0], None)
            odd[0] = (a[0] - b[0], None)
        elif 2 * k == half:
            even[k] = (a[0] + a[0], None)
            odd[k] = (-(a[1] + a[1]), None)
        else:
            angle = 2.0 * math.pi * k / n
            even[k] = (a[0] + b[0], a[1] - b[1])
            odd[k] = times((a[0] - b[0], a[1] + b[1]), math.cos(angle), math.sin(angle))
    out = [None] * n
    out[0::2] = real_inverse(even)
    out[1::2] = real_inverse(odd)
    return out


def kernel(
    pix, chan, sky_ref, flags_ref, modes_ref, block_ref, offset_ref, weight_ref, table_ref, twiddle_ref,
    out_ref, stack_ref,
    lines, flags, modes_v, block_v, offset_v, weights, chosen_w, meta, meta_own, meta_smem, table, twiddle, spec, kept, back, cube, staged,
    part, sums, part2, sums2, flag_f, mask_ref, local_sem, out_sem, line_send, line_recv, flag_send, flag_recv,
    w_send, w_recv, m_send, m_recv, s_send, s_recv, t_send, t_recv,
):
    me_p, me_c = lax.axis_index("pix"), lax.axis_index("chan")
    rows = lines.shape[1]
    per = SLABS // chan
    count = weights.shape[1]
    patch = weights.shape[2]
    steps = rows // STEP

    barrier = pltpu.get_barrier_semaphore()
    chan_peers = [lax.rem(me_c + d, chan) for d in range(1, chan)]
    pix_peers = [lax.rem(me_p + d, pix) for d in range(1, pix)]
    for c in chan_peers:
        pl.semaphore_signal(barrier, inc=1, device_id=(me_p, c), device_id_type=MESH)
    for p in pix_peers:
        pl.semaphore_signal(barrier, inc=1, device_id=(p, me_c), device_id_type=MESH)

    own = [
        pltpu.make_async_copy(table_ref, table, local_sem.at[0]),
        pltpu.make_async_copy(sky_ref.at[pl.ds(pl.multiple_of(me_c * rows, rows), rows)], lines.at[me_c], local_sem.at[1]),
        pltpu.make_async_copy(flags_ref, flags.at[me_c], local_sem.at[2]),
        pltpu.make_async_copy(weight_ref, weights.at[me_p], local_sem.at[3]),
        pltpu.make_async_copy(modes_ref, modes_v, local_sem.at[5]),
        pltpu.make_async_copy(twiddle_ref, twiddle, local_sem.at[8]),
    ]
    places = [
        pltpu.make_async_copy(block_ref, block_v, local_sem.at[6]),
        pltpu.make_async_copy(offset_ref, offset_v, local_sem.at[7]),
    ]
    for copy in places + own:
        copy.start()
    for copy in places:
        copy.wait()
    meta_own[0:1, 0:count] = block_v[...]
    meta_own[1:2, 0:count] = offset_v[...]
    pl.semaphore_wait(barrier, chan + pix - 2)

    def remote(src, dst, send, recv, device):
        return pltpu.make_async_remote_copy(
            src_ref=src, dst_ref=dst, send_sem=send, recv_sem=recv, device_id=device, device_id_type=MESH
        )

    def line_copy(i, c, step):
        there = pl.ds(pl.multiple_of(c * rows + step * STEP, STEP), STEP)
        here = pl.ds(pl.multiple_of(step * STEP, STEP), STEP)
        return remote(
            sky_ref.at[there], lines.at[me_c, here], line_send.at[step, i], line_recv.at[step, i], (me_p, c)
        )

    flag_copies, w_copies, m_copies = [], [], []
    for step in range(steps):
        for i, c in enumerate(chan_peers):
            if step == 0:
                flag_copies.append(remote(flags_ref, flags.at[me_c], flag_send.at[i], flag_recv.at[i], (me_p, c)))
                flag_copies[-1].start()
            line_copy(i, c, step).start()
    for i, p in enumerate(pix_peers):
        m_copies.append(remote(meta_own, meta.at[me_p], m_send.at[i], m_recv.at[i], (p, me_c)))
        m_copies[-1].start()
        w_copies.append(remote(weight_ref, weights.at[me_p], w_send.at[i], w_recv.at[i], (p, me_c)))
        w_copies[-1].start()

    for copy in own:
        copy.wait()
    modes = modes_v[...].astype(jnp.float32)
    eye = (
        lax.broadcasted_iota(jnp.int32, (LANES, LANES), 0) == lax.broadcasted_iota(jnp.int32, (LANES, LANES), 1)
    ).astype(jnp.float32)
    turned = lax.dot_general(eye, modes, (((1,), (1,)), ((), ())), preferred_element_type=jnp.float32)
    mask = jnp.zeros((32, LANES), jnp.float32)
    for q in range(4):
        place = (
            lax.broadcasted_iota(jnp.int32, (32, LANES), 1) == lax.broadcasted_iota(jnp.int32, (32, LANES), 0) + 32 * q
        ).astype(jnp.float32)
        mask = mask + jnp.dot(turned[32 * q : 32 * q + 32], place, preferred_element_type=jnp.float32)
    for k in range(HALF):
        other = HALF if k == 0 else SLABS - k
        gain = 1.0 if k == 0 else 0.5
        mask_ref[k : k + 1, :LANES] = mask[k : k + 1] * gain
        mask_ref[k : k + 1, LANES:] = mask[other : other + 1] * gain

    for copy in flag_copies:
        copy.wait()
    for c in range(chan):
        flag_f[c * per : (c + 1) * per, :] = flags[c].astype(jnp.float32)

    def slab(n1, at):
        c, s = n1 // per, n1 % per
        value = lines[c, pl.ds(at, CHUNK), s * LANES : (s + 1) * LANES].astype(jnp.float32)
        return value * flag_f[n1 : n1 + 1, :]

    def filter_rows(step, carry):
        for i, c in enumerate(chan_peers):
            line_copy(i, c, step).wait_recv()
        for j in range(STEP // CHUNK):
            at = pl.multiple_of(step * STEP + j * CHUNK, CHUNK)
            r = slice(j * CHUNK, (j + 1) * CHUNK)
            y = real_forward([slab(n1, at) for n1 in range(SLABS)])
            spec[0, r, :LANES] = y[0][0].astype(jnp.bfloat16)
            spec[0, r, LANES:] = y[HALF][0].astype(jnp.bfloat16)
            for k in range(1, HALF):
                (re, im), cos, sin = y[k], twiddle[k : k + 1], twiddle[HALF + k : HALF + k + 1]
                spec[k, r, :LANES] = (re * cos + im * sin).astype(jnp.bfloat16)
                spec[k, r, LANES:] = (im * cos - re * sin).astype(jnp.bfloat16)
        def stretch(ref, lo, hi):
            return ref[lo:hi].reshape((hi - lo) * STEP, 2 * LANES)

        for which, lo, hi in ((0, 0, 1), (1, 1, HALF)):
            coeffs = jnp.dot(stretch(spec, lo, hi), table[which], preferred_element_type=jnp.float32)
            for k in range(lo, hi):
                mine = coeffs[(k - lo) * STEP : (k - lo + 1) * STEP]
                kept[k] = (mine * mask_ref[k : k + 1]).astype(jnp.bfloat16)
            ripple = jnp.dot(stretch(kept, lo, hi), table[2 + which], preferred_element_type=jnp.float32)
            back[lo:hi] = ripple.reshape(hi - lo, STEP, 2 * LANES)
        for j in range(STEP // CHUNK):
            at = pl.multiple_of(step * STEP + j * CHUNK, CHUNK)
            r = slice(j * CHUNK, (j + 1) * CHUNK)
            z = [(back[0, r, :LANES], None)]
            for k in range(1, HALF):
                re, im = back[k, r, :LANES], back[k, r, LANES:]
                cos, sin = twiddle[k : k + 1], twiddle[HALF + k : HALF + k + 1]
                z.append((re * cos - im * sin, re * sin + im * cos))
            z += [(back[0, r, LANES:], None)]
            ripple = real_inverse(z)
            for n1 in range(SLABS):
                value = (slab(n1, at) - ripple[n1]).astype(jnp.bfloat16)
                staged[pl.ds(at, CHUNK), n1 * LANES : (n1 + 1) * LANES] = value
                cube[(step * (STEP // CHUNK) + j) * SLABS + n1] = value.astype(jnp.float32)
        here = pl.ds(pl.multiple_of(step * STEP, STEP), STEP)
        pltpu.make_async_copy(staged.at[here], out_ref.at[here], out_sem.at[step]).start()
        return carry

    lax.fori_loop(0, steps - 1, filter_rows, 0)

    meta[me_p] = meta_own[...]
    for copy in m_copies:
        copy.wait()
    to_smem = pltpu.make_async_copy(meta, meta_smem, local_sem.at[4])
    to_smem.start()
    for copy in w_copies:
        copy.wait()
    to_smem.wait()

    here_blocks = rows // patch
    first = (me_p * chan + me_c) * here_blocks

    def choose(p, acc):
        for g in range(count):
            local = meta_smem[p, 0, g] - first
            safe = jnp.clip(local, 0, here_blocks - 1)
            offset = meta_smem[p, 1, g]
            base = lax.div(offset, LANES)
            shift = offset - base * LANES
            meta_smem[p, 2, g] = safe * SLABS + base
            meta_smem[p, 3, g] = safe * SLABS + jnp.minimum(base + 1, SLABS - 1)
            meta_smem[p, 4, g] = shift
            w = weights[p, g].astype(jnp.float32)
            acc = acc + w * w
            chosen_w[p, g] = jnp.where(local == safe, w, 0.0)
        return acc

    power = lax.fori_loop(0, pix, choose, jnp.zeros((patch, LANES), jnp.float32))

    filter_rows(steps - 1, 0)

    lane = lax.broadcasted_iota(jnp.int32, (patch, LANES), 1)

    def add_panels(p, acc):
        for g in range(count):
            low = cube[meta_smem[p, 2, g]]
            high = cube[meta_smem[p, 3, g]]
            shift = meta_smem[p, 4, g]
            joined = jnp.where(lane >= shift, low, high)
            panel = pltpu.roll(joined, lax.rem(LANES - shift, LANES), 1)
            acc = acc + chosen_w[p, g] * panel
        return acc

    total = lax.fori_loop(0, pix, add_panels, jnp.zeros((patch, LANES), jnp.float32))

    part[...] = total
    sends = [
        remote(part, sums.at[me_p], s_send.at[i], s_recv.at[i], (p, me_c)) for i, p in enumerate(pix_peers)
    ]
    for copy in sends:
        copy.start()
    sums[me_p] = total
    for copy in sends:
        copy.wait()
    total = jnp.sum(sums[...], axis=0)
    part2[...] = total
    sends = [
        remote(part2, sums2.at[me_c], t_send.at[i], t_recv.at[i], (me_p, c)) for i, c in enumerate(chan_peers)
    ]
    for copy in sends:
        copy.start()
    sums2[me_c] = total
    for step in range(steps):
        for i, c in enumerate(chan_peers):
            line_copy(i, c, step).wait_send()
        here = pl.ds(step * STEP, STEP)
        pltpu.make_async_copy(staged.at[here], out_ref.at[here], out_sem.at[step]).wait()
    for copy in sends:
        copy.wait()
    stack_ref[...] = jnp.sum(sums2[...], axis=0) / jnp.sqrt(power)


def hand_over(filtered_ref, stack_ref, out_ref, stack_out, sem):
    copy = pltpu.make_async_copy(filtered_ref, out_ref, sem)
    copy.start()
    stack_out[...] = stack_ref[...]
    copy.wait()


def solution(mesh):
    pix, chan = mesh.shape["pix"], mesh.shape["chan"]

    def body(sky_map, channel_flags, ripple_modes, galaxy_block, galaxy_offset, galaxy_weight):
        rows = sky_map.shape[0] // chan
        width = sky_map.shape[1]
        count, patch, _ = galaxy_weight.shape
        per = width // LANES
        any_spec = pl.BlockSpec(memory_space=pl.ANY)
        vmem_spec = pl.BlockSpec(memory_space=pltpu.VMEM)
        dma = pltpu.SemaphoreType.DMA
        table, twiddle = (jnp.asarray(v) for v in mode_tables())
        shapes = (
            jax.ShapeDtypeStruct((rows, TOTAL), jnp.bfloat16),
            jax.ShapeDtypeStruct((patch, LANES), jnp.float32),
        )
        filtered, stack = pl.pallas_call(
            functools.partial(kernel, pix, chan),
            out_shape=shapes,
            in_specs=[pl.BlockSpec(memory_space=pltpu.HBM)] * 8,
            out_specs=(any_spec, vmem_spec),
            scratch_shapes=[
                pltpu.VMEM((chan, rows, width), jnp.bfloat16),
                pltpu.VMEM((chan, per, LANES), jnp.int32),
                pltpu.VMEM((32, LANES), jnp.int32),
                pltpu.VMEM((1, count), jnp.int32),
                pltpu.VMEM((1, count), jnp.int32),
                pltpu.VMEM((pix, count, patch, LANES), jnp.bfloat16),
                pltpu.VMEM((pix, count, patch, LANES), jnp.float32),
                pltpu.VMEM((pix, 8, LANES), jnp.int32),
                pltpu.VMEM((8, LANES), jnp.int32),
                pltpu.SMEM((pix, 8, LANES), jnp.int32),
                pltpu.VMEM((4, 2 * LANES, 2 * LANES), jnp.bfloat16),
                pltpu.VMEM((SLABS, LANES), jnp.float32),
                pltpu.VMEM((HALF, STEP, 2 * LANES), jnp.bfloat16),
                pltpu.VMEM((HALF, STEP, 2 * LANES), jnp.bfloat16),
                pltpu.VMEM((HALF, STEP, 2 * LANES), jnp.float32),
                pltpu.VMEM((rows // patch * SLABS, patch, LANES), jnp.float32),
                pltpu.VMEM((rows, TOTAL), jnp.bfloat16),
                pltpu.VMEM((patch, LANES), jnp.float32),
                pltpu.VMEM((pix, patch, LANES), jnp.float32),
                pltpu.VMEM((patch, LANES), jnp.float32),
                pltpu.VMEM((chan, patch, LANES), jnp.float32),
                pltpu.VMEM((SLABS, LANES), jnp.float32),
                pltpu.VMEM((HALF, 2 * LANES), jnp.float32),
                dma((9,)), dma((rows // STEP,)),
                dma((rows // STEP, chan - 1)), dma((rows // STEP, chan - 1)), dma((chan - 1,)), dma((chan - 1,)),
                dma((pix - 1,)), dma((pix - 1,)), dma((pix - 1,)), dma((pix - 1,)),
                dma((pix - 1,)), dma((pix - 1,)),
                dma((chan - 1,)), dma((chan - 1,)),
            ],
            compiler_params=pltpu.CompilerParams(collective_id=0, has_side_effects=True, vmem_limit_bytes=32 << 20),
        )(
            *(pltpu.with_memory_space_constraint(v, pltpu.HBM) for v in (
            sky_map, channel_flags.reshape(per, LANES), ripple_modes.reshape(32, LANES),
            galaxy_block.reshape(1, count), galaxy_offset.reshape(1, count), galaxy_weight, table, twiddle,
            ))
        )
        return pl.pallas_call(
            hand_over,
            out_shape=shapes,
            in_specs=[any_spec, vmem_spec],
            out_specs=(any_spec, vmem_spec),
            scratch_shapes=[dma(())],
            compiler_params=pltpu.CompilerParams(vmem_limit_bytes=2 << 20),
        )(filtered, stack)

    in_specs = (P("pix", "chan"), P("chan"), P(), P("pix"), P("pix"), P("pix", None, None))
    out_specs = (P(("pix", "chan"), None), P())
    return jax.shard_map(body, mesh=mesh, in_specs=in_specs, out_specs=out_specs, check_vma=False)
```

```python
import functools
import math

import jax
import jax.numpy as jnp
import numpy as np
from jax import lax
from jax.experimental import pallas as pl
from jax.experimental.pallas import tpu as pltpu
from jax.sharding import PartitionSpec as P

MESH = pl.DeviceIdType.MESH
LANES = 128
SLABS = 32
TOTAL = LANES * SLABS
HALF = SLABS // 2
CHUNK = 16
STEP = 64


def mode_tables():
    col = np.arange(LANES)
    quarter, row = col // 32, col % 32
    is_sin, k2 = (row // 16 == 1)[None, :], 4 * (row % 16) + quarter
    lane = np.arange(LANES)[:, None]

    def waves(k):
        phase = 2.0 * np.pi * ((lane * k[None, :]) % TOTAL) / TOTAL
        return np.cos(phase) * math.sqrt(2.0 / TOTAL), np.sin(phase) * math.sqrt(2.0 / TOTAL)

    tables = np.zeros((4, 2 * LANES, 2 * LANES))
    cos, sin = waves(32 * k2)
    cos[:, k2 == 0] *= math.sqrt(0.5)
    sin[:, k2 == 0] = np.where(lane % 2 == 0, 1.0, -1.0) * math.sqrt(1.0 / TOTAL)
    tables[0, :LANES, :LANES] = np.where(is_sin, sin, cos)
    cos, sin = waves(32 * k2 + 16)
    tables[0, LANES:, LANES:] = np.where(is_sin, sin, cos)
    cos, sin = waves(32 * k2)
    tables[1, :LANES, :LANES] = np.where(is_sin, sin, cos)
    tables[1, LANES:, :LANES] = np.where(is_sin, -cos, sin)
    cos, sin = waves(32 * (LANES - 1 - k2))
    tables[1, :LANES, LANES:] = np.where(is_sin, -sin, cos)
    tables[1, LANES:, LANES:] = np.where(is_sin, cos, sin)
    tables[2], tables[3] = tables[0].T, tables[1].T
    phase = 2.0 * np.pi * np.arange(HALF)[:, None] * np.arange(LANES)[None, :] / TOTAL
    return tables.astype(jnp.bfloat16), np.concatenate([np.cos(phase), np.sin(phase)]).astype(np.float32)


def times(value, c, s):
    re, im = value
    eps = 1e-12
    if abs(s) < eps and abs(c - 1) < eps:
        return value
    if abs(c) < eps and abs(s - 1) < eps:
        return (-im, re)
    if abs(c) < eps and abs(s + 1) < eps:
        return (im, -re)
    if abs(abs(c) - abs(s)) < eps:
        a = abs(c)
        sc, ss = math.copysign(1, c), math.copysign(1, s)
        t = re * (a * sc)
        u = im * (a * sc)
        return (t - u, u + t) if sc == ss else (t + u, u - t)
    return (re * c - im * s, re * s + im * c)


def real_forward(x):
    n = len(x)
    if n == 2:
        return [(x[0] + x[1], None), (x[0] - x[1], None)]
    even, odd = real_forward(x[0::2]), real_forward(x[1::2])
    half = n // 2
    out = [None] * (half + 1)
    for k in range(half // 2 + 1):
        e, o = even[k], odd[k]
        if k == 0:
            out[0] = (e[0] + o[0], None)
            out[half] = (e[0] - o[0], None)
        elif 2 * k == half:
            out[k] = (e[0], -o[0])
        else:
            angle = -2.0 * math.pi * k / n
            tr, ti = times(o, math.cos(angle), math.sin(angle))
            out[k] = (e[0] + tr, e[1] + ti)
            out[half - k] = (e[0] - tr, ti - e[1])
    return out


def real_inverse(z):
    half = len(z) - 1
    n = 2 * half
    if n == 2:
        return [z[0][0] + z[1][0], z[0][0] - z[1][0]]
    even, odd = [None] * (half // 2 + 1), [None] * (half // 2 + 1)
    for k in range(half // 2 + 1):
        a, b = z[k], z[half - k]
        if k == 0:
            even[0] = (a[0] + b[0], None)
            odd[0] = (a[0] - b[0], None)
        elif 2 * k == half:
            even[k] = (a[0] + a[0], None)
            odd[k] = (-(a[1] + a[1]), None)
        else:
            angle = 2.0 * math.pi * k / n
            even[k] = (a[0] + b[0], a[1] - b[1])
            odd[k] = times((a[0] - b[0], a[1] + b[1]), math.cos(angle), math.sin(angle))
    out = [None] * n
    out[0::2] = real_inverse(even)
    out[1::2] = real_inverse(odd)
    return out


def partners(me, size):
    if size & (size - 1):
        return [lax.rem(me + d, size) for d in range(1, size)]
    found = []
    for d in range(size - 1, 0, -1):
        at, bit = me, 1
        while bit < size:
            if d & bit:
                at = at + bit * (1 - 2 * lax.rem(lax.div(at, bit), 2))
            bit *= 2
        found.append(at)
    return found


def kernel(
    pix, chan, sky_ref, flags_ref, modes_ref, block_ref, offset_ref, weight_ref, table_ref, twiddle_ref,
    out_ref, stack_ref,
    lines, flags, modes_v, block_v, offset_v, weights, chosen_w, meta, meta_own, meta_smem, table, twiddle, spec, kept, back, cube, staged,
    part, sums, part2, sums2, flag_f, mask_ref, local_sem, out_sem, line_send, line_recv, flag_send, flag_recv,
    w_send, w_recv, m_send, m_recv, s_send, s_recv, t_send, t_recv,
):
    me_p, me_c = lax.axis_index("pix"), lax.axis_index("chan")
    rows = lines.shape[1]
    per = SLABS // chan
    count = weights.shape[1]
    patch = weights.shape[2]
    steps = rows // STEP

    barrier = pltpu.get_barrier_semaphore()
    chan_peers = partners(me_c, chan)
    pix_peers = partners(me_p, pix)
    for c in chan_peers:
        pl.semaphore_signal(barrier, inc=1, device_id=(me_p, c), device_id_type=MESH)
    for p in pix_peers:
        pl.semaphore_signal(barrier, inc=1, device_id=(p, me_c), device_id_type=MESH)

    own = [
        pltpu.make_async_copy(table_ref, table, local_sem.at[0]),
        pltpu.make_async_copy(sky_ref.at[pl.ds(pl.multiple_of(me_c * rows, rows), rows)], lines.at[me_c], local_sem.at[1]),
        pltpu.make_async_copy(flags_ref, flags.at[me_c], local_sem.at[2]),
        pltpu.make_async_copy(weight_ref, weights.at[me_p], local_sem.at[3]),
        pltpu.make_async_copy(modes_ref, modes_v, local_sem.at[5]),
        pltpu.make_async_copy(twiddle_ref, twiddle, local_sem.at[8]),
    ]
    places = [
        pltpu.make_async_copy(block_ref, block_v, local_sem.at[6]),
        pltpu.make_async_copy(offset_ref, offset_v, local_sem.at[7]),
    ]
    for copy in places + own:
        copy.start()
    for copy in places:
        copy.wait()
    meta_own[0:1, 0:count] = block_v[...]
    meta_own[1:2, 0:count] = offset_v[...]
    pl.semaphore_wait(barrier, chan + pix - 2)

    def remote(src, dst, send, recv, device):
        return pltpu.make_async_remote_copy(
            src_ref=src, dst_ref=dst, send_sem=send, recv_sem=recv, device_id=device, device_id_type=MESH
        )

    def line_copy(i, c, step):
        there = pl.ds(pl.multiple_of(c * rows + step * STEP, STEP), STEP)
        here = pl.ds(pl.multiple_of(step * STEP, STEP), STEP)
        return remote(
            sky_ref.at[there], lines.at[me_c, here], line_send.at[step, i], line_recv.at[step, i], (me_p, c)
        )

    flag_copies, w_copies, m_copies = [], [], []
    for step in range(steps):
        for i, c in enumerate(chan_peers):
            if step == 0:
                flag_copies.append(remote(flags_ref, flags.at[me_c], flag_send.at[i], flag_recv.at[i], (me_p, c)))
                flag_copies[-1].start()
            line_copy(i, c, step).start()
    for i, p in enumerate(pix_peers):
        m_copies.append(remote(meta_own, meta.at[me_p], m_send.at[i], m_recv.at[i], (p, me_c)))
        m_copies[-1].start()
        w_copies.append(remote(weight_ref, weights.at[me_p], w_send.at[i], w_recv.at[i], (p, me_c)))
        w_copies[-1].start()

    for copy in own:
        copy.wait()
    modes = modes_v[...].astype(jnp.float32)
    eye = (
        lax.broadcasted_iota(jnp.int32, (LANES, LANES), 0) == lax.broadcasted_iota(jnp.int32, (LANES, LANES), 1)
    ).astype(jnp.float32)
    turned = lax.dot_general(eye, modes, (((1,), (1,)), ((), ())), preferred_element_type=jnp.float32)
    mask = jnp.zeros((32, LANES), jnp.float32)
    for q in range(4):
        place = (
            lax.broadcasted_iota(jnp.int32, (32, LANES), 1) == lax.broadcasted_iota(jnp.int32, (32, LANES), 0) + 32 * q
        ).astype(jnp.float32)
        mask = mask + jnp.dot(turned[32 * q : 32 * q + 32], place, preferred_element_type=jnp.float32)
    for k in range(HALF):
        other = HALF if k == 0 else SLABS - k
        gain = 1.0 if k == 0 else 0.5
        mask_ref[k : k + 1, :LANES] = mask[k : k + 1] * gain
        mask_ref[k : k + 1, LANES:] = mask[other : other + 1] * gain

    for copy in flag_copies:
        copy.wait()
    for c in range(chan):
        flag_f[c * per : (c + 1) * per, :] = flags[c].astype(jnp.float32)

    def slab(n1, at):
        c, s = n1 // per, n1 % per
        value = lines[c, pl.ds(at, CHUNK), s * LANES : (s + 1) * LANES].astype(jnp.float32)
        return value * flag_f[n1 : n1 + 1, :]

    def filter_rows(step, carry):
        for i, c in enumerate(chan_peers):
            line_copy(i, c, step).wait_recv()
        for j in range(STEP // CHUNK):
            at = pl.multiple_of(step * STEP + j * CHUNK, CHUNK)
            r = slice(j * CHUNK, (j + 1) * CHUNK)
            y = real_forward([slab(n1, at) for n1 in range(SLABS)])
            spec[0, r, :LANES] = y[0][0].astype(jnp.bfloat16)
            spec[0, r, LANES:] = y[HALF][0].astype(jnp.bfloat16)
            for k in range(1, HALF):
                (re, im), cos, sin = y[k], twiddle[k : k + 1], twiddle[HALF + k : HALF + k + 1]
                spec[k, r, :LANES] = (re * cos + im * sin).astype(jnp.bfloat16)
                spec[k, r, LANES:] = (im * cos - re * sin).astype(jnp.bfloat16)
        def stretch(ref, lo, hi):
            return ref[lo:hi].reshape((hi - lo) * STEP, 2 * LANES)

        for which, lo, hi in ((0, 0, 1), (1, 1, HALF)):
            coeffs = jnp.dot(stretch(spec, lo, hi), table[which], preferred_element_type=jnp.float32)
            for k in range(lo, hi):
                mine = coeffs[(k - lo) * STEP : (k - lo + 1) * STEP]
                kept[k] = (mine * mask_ref[k : k + 1]).astype(jnp.bfloat16)
            ripple = jnp.dot(stretch(kept, lo, hi), table[2 + which], preferred_element_type=jnp.float32)
            back[lo:hi] = ripple.reshape(hi - lo, STEP, 2 * LANES)
        for j in range(STEP // CHUNK):
            at = pl.multiple_of(step * STEP + j * CHUNK, CHUNK)
            r = slice(j * CHUNK, (j + 1) * CHUNK)
            z = [(back[0, r, :LANES], None)]
            for k in range(1, HALF):
                re, im = back[k, r, :LANES], back[k, r, LANES:]
                cos, sin = twiddle[k : k + 1], twiddle[HALF + k : HALF + k + 1]
                z.append((re * cos - im * sin, re * sin + im * cos))
            z += [(back[0, r, LANES:], None)]
            ripple = real_inverse(z)
            for n1 in range(SLABS):
                value = (slab(n1, at) - ripple[n1]).astype(jnp.bfloat16)
                staged[pl.ds(at, CHUNK), n1 * LANES : (n1 + 1) * LANES] = value
                cube[(step * (STEP // CHUNK) + j) * SLABS + n1] = value.astype(jnp.float32)
        here = pl.ds(pl.multiple_of(step * STEP, STEP), STEP)
        pltpu.make_async_copy(staged.at[here], out_ref.at[here], out_sem.at[step]).start()
        return carry

    lax.fori_loop(0, steps - 1, filter_rows, 0)

    meta[me_p] = meta_own[...]
    for copy in m_copies:
        copy.wait()
    to_smem = pltpu.make_async_copy(meta, meta_smem, local_sem.at[4])
    to_smem.start()
    for copy in w_copies:
        copy.wait()
    to_smem.wait()

    here_blocks = rows // patch
    first = (me_p * chan + me_c) * here_blocks

    def choose(p, acc):
        for g in range(count):
            local = meta_smem[p, 0, g] - first
            safe = jnp.clip(local, 0, here_blocks - 1)
            offset = meta_smem[p, 1, g]
            base = lax.div(offset, LANES)
            shift = offset - base * LANES
            meta_smem[p, 2, g] = safe * SLABS + base
            meta_smem[p, 3, g] = safe * SLABS + jnp.minimum(base + 1, SLABS - 1)
            meta_smem[p, 4, g] = shift
            meta_smem[p, 5, g] = lax.rem(LANES - shift, LANES)
            w = weights[p, g].astype(jnp.float32)
            acc = acc + w * w
            chosen_w[p, g] = jnp.where(local == safe, w, 0.0)
        return acc

    power = lax.fori_loop(0, pix, choose, jnp.zeros((patch, LANES), jnp.float32))

    filter_rows(steps - 1, 0)

    lane = lax.broadcasted_iota(jnp.int32, (patch, LANES), 1)

    def add_panels(p, acc):
        for g in range(count):
            low = cube[meta_smem[p, 2, g]]
            high = cube[meta_smem[p, 3, g]]
            shift = meta_smem[p, 4, g]
            joined = jnp.where(lane >= shift, low, high)
            panel = pltpu.roll(joined, meta_smem[p, 5, g], 1)
            acc = acc + chosen_w[p, g] * panel
        return acc

    total = lax.fori_loop(0, pix, add_panels, jnp.zeros((patch, LANES), jnp.float32))

    part[...] = total
    sends = [
        remote(part, sums.at[me_p], s_send.at[i], s_recv.at[i], (p, me_c)) for i, p in enumerate(pix_peers)
    ]
    for copy in sends:
        copy.start()
    sums[me_p] = total
    for copy in sends:
        copy.wait()
    total = jnp.sum(sums[...], axis=0)
    part2[...] = total
    sends = [
        remote(part2, sums2.at[me_c], t_send.at[i], t_recv.at[i], (me_p, c)) for i, c in enumerate(chan_peers)
    ]
    for copy in sends:
        copy.start()
    sums2[me_c] = total
    for step in range(steps):
        for i, c in enumerate(chan_peers):
            line_copy(i, c, step).wait_send()
        here = pl.ds(step * STEP, STEP)
        pltpu.make_async_copy(staged.at[here], out_ref.at[here], out_sem.at[step]).wait()
    for copy in sends:
        copy.wait()
    stack_ref[...] = jnp.sum(sums2[...], axis=0) / jnp.sqrt(power)


def hand_over(filtered_ref, stack_ref, out_ref, stack_out, sem):
    copy = pltpu.make_async_copy(filtered_ref, out_ref, sem)
    copy.start()
    stack_out[...] = stack_ref[...]
    copy.wait()


def solution(mesh):
    pix, chan = mesh.shape["pix"], mesh.shape["chan"]

    def body(sky_map, channel_flags, ripple_modes, galaxy_block, galaxy_offset, galaxy_weight):
        rows = sky_map.shape[0] // chan
        width = sky_map.shape[1]
        count, patch, _ = galaxy_weight.shape
        per = width // LANES
        any_spec = pl.BlockSpec(memory_space=pl.ANY)
        vmem_spec = pl.BlockSpec(memory_space=pltpu.VMEM)
        dma = pltpu.SemaphoreType.DMA
        table, twiddle = (jnp.asarray(v) for v in mode_tables())
        shapes = (
            jax.ShapeDtypeStruct((rows, TOTAL), jnp.bfloat16),
            jax.ShapeDtypeStruct((patch, LANES), jnp.float32),
        )
        filtered, stack = pl.pallas_call(
            functools.partial(kernel, pix, chan),
            out_shape=shapes,
            in_specs=[pl.BlockSpec(memory_space=pltpu.HBM)] * 8,
            out_specs=(any_spec, vmem_spec),
            scratch_shapes=[
                pltpu.VMEM((chan, rows, width), jnp.bfloat16),
                pltpu.VMEM((chan, per, LANES), jnp.int32),
                pltpu.VMEM((32, LANES), jnp.int32),
                pltpu.VMEM((1, count), jnp.int32),
                pltpu.VMEM((1, count), jnp.int32),
                pltpu.VMEM((pix, count, patch, LANES), jnp.bfloat16),
                pltpu.VMEM((pix, count, patch, LANES), jnp.float32),
                pltpu.VMEM((pix, 8, LANES), jnp.int32),
                pltpu.VMEM((8, LANES), jnp.int32),
                pltpu.SMEM((pix, 8, LANES), jnp.int32),
                pltpu.VMEM((4, 2 * LANES, 2 * LANES), jnp.bfloat16),
                pltpu.VMEM((SLABS, LANES), jnp.float32),
                pltpu.VMEM((HALF, STEP, 2 * LANES), jnp.bfloat16),
                pltpu.VMEM((HALF, STEP, 2 * LANES), jnp.bfloat16),
                pltpu.VMEM((HALF, STEP, 2 * LANES), jnp.float32),
                pltpu.VMEM((rows // patch * SLABS, patch, LANES), jnp.float32),
                pltpu.VMEM((rows, TOTAL), jnp.bfloat16),
                pltpu.VMEM((patch, LANES), jnp.float32),
                pltpu.VMEM((pix, patch, LANES), jnp.float32),
                pltpu.VMEM((patch, LANES), jnp.float32),
                pltpu.VMEM((chan, patch, LANES), jnp.float32),
                pltpu.VMEM((SLABS, LANES), jnp.float32),
                pltpu.VMEM((HALF, 2 * LANES), jnp.float32),
                dma((9,)), dma((rows // STEP,)),
                dma((rows // STEP, chan - 1)), dma((rows // STEP, chan - 1)), dma((chan - 1,)), dma((chan - 1,)),
                dma((pix - 1,)), dma((pix - 1,)), dma((pix - 1,)), dma((pix - 1,)),
                dma((pix - 1,)), dma((pix - 1,)),
                dma((chan - 1,)), dma((chan - 1,)),
            ],
            compiler_params=pltpu.CompilerParams(collective_id=0, has_side_effects=True, vmem_limit_bytes=32 << 20),
        )(
            *(pltpu.with_memory_space_constraint(v, pltpu.HBM) for v in (
            sky_map, channel_flags.reshape(per, LANES), ripple_modes.reshape(32, LANES),
            galaxy_block.reshape(1, count), galaxy_offset.reshape(1, count), galaxy_weight, table, twiddle,
            ))
        )
        return pl.pallas_call(
            hand_over,
            out_shape=shapes,
            in_specs=[any_spec, vmem_spec],
            out_specs=(any_spec, vmem_spec),
            scratch_shapes=[dma(())],
            compiler_params=pltpu.CompilerParams(vmem_limit_bytes=2 << 20),
        )(filtered, stack)

    in_specs = (P("pix", "chan"), P("chan"), P(), P("pix"), P("pix"), P("pix", None, None))
    out_specs = (P(("pix", "chan"), None), P())
    return jax.shard_map(body, mesh=mesh, in_specs=in_specs, out_specs=out_specs, check_vma=False)
```
